768 devices in a mesh: elem: 128 (over x, y, z_hi, core), state: 6 (over z_lo).
Axes of the slice: x: 4, y: 8, z: 12 (z_hi: 2, z_lo: 6; z = z_hi * 6 + z_lo), core: 2. Of those that a mesh axis runs over, the one named last changes fastest.
Arguments:
- orbitals: bfloat16 [1536, 160, 768], P(('elem', 'state')), may hold values from -6 to 6
- rotation: bfloat16 [768, 768], replicated, may hold values from -0.21875 to 0.21875
- counts: int32 [1536], P('elem'), may hold values from 96 to 160, as said below
- neighbors: int32 [1536, 5], P('elem'), may hold values from 0 to 1535, as said below
- blocks: bfloat16 [1536, 5, 160, 160], P('elem'), may hold values from -0.21875 to 0.21875
Outputs:
- filtered: bfloat16 [1536, 160, 768], P(('elem', 'state'))
The draws below stay inside these ranges and needn't reach their ends.
Inputs may be any that keep to these rules, and one draw needn't show every extreme that they name: `neighbors`: entry 0 of row e is e; every other entry is (e + d) mod 1536 with 1 <= |d| <= 4. The adaptive basis is sized per pair of neighbouring elements: over each aligned block of 2 elements the counts sum to at most 288, and the first block of every index of elem sums to exactly 288.
All inputs are finite; a program needn't handle non-finite values.
Results may differ from the reference program's by a relative error of at most 0.007.
Values may be sent and summed in bfloat16 or wider, within the bound.
A program may use at most 64 MiB of HBM per device.

```python
import jax
import jax.numpy as jnp
from jax import lax

NB = 160
E_LOC = 12
DEG = 4
REACH = 4
ER = 2
E = 1536
NS = 768
N_ELEM = 128


def draw_neighbors(key, part):
    distance = jax.random.randint(jax.random.fold_in(key, 11), (E, 4), 1, REACH + 1)
    direction = jax.random.randint(jax.random.fold_in(key, 12), (E, 4), 0, 2) * 2 - 1
    itself = jnp.arange(E, dtype=jnp.int32)[:, None]
    others = jnp.mod(itself + distance * direction, E)
    return jnp.concatenate([itself, others], axis=1).astype(jnp.int32)


def draw_counts(key, part):
    base_count = NB * 3 // 5
    cap_elem = NB * 9 // 10
    budget = ER * (cap_elem - base_count)
    extra = jax.random.randint(jax.random.fold_in(key, 21), (E // ER, ER), 0, NB - base_count + 1)
    before = jnp.cumsum(extra, axis=1) - extra
    clipped = jnp.minimum(extra, jnp.maximum(budget - before, 0))
    first_extra = min(budget, NB - base_count)
    rest_extra = budget - first_extra
    others = max(ER - 1, 1)
    lanes = jnp.arange(ER, dtype=jnp.int32)
    spread = rest_extra // others + (lanes - 1 < rest_extra % others).astype(jnp.int32)
    forced = jnp.where(lanes == 0, first_extra, spread)
    block_ids = jnp.arange(E // ER, dtype=jnp.int32)
    is_first = block_ids * ER % E_LOC == 0
    final_extra = jnp.where(is_first[:, None], forced[None, :], clipped)
    return (base_count + final_extra).reshape(E).astype(jnp.int32)


def block_levels(own_key, shape, cuts, smallest, high):
    loudness, own = 1.0, jax.random.fold_in(own_key, 6)
    for axis_at, parts in cuts:
        draws = jnp.exp(jax.random.uniform(jax.random.fold_in(own, axis_at), (parts,), jnp.float32, smallest / len(cuts), high / len(cuts)))
        loudness = loudness * jnp.repeat(draws, shape[axis_at] // parts).reshape([-1 if axis == axis_at else 1 for axis in range(len(shape))])
    return loudness


def noise(rng, extent, width, bound, cuts=(), held_as=jnp.bfloat16):
    values = jax.random.normal(rng, extent, jnp.float32) * width
    if len(cuts) > 0:
        values = block_levels(rng, extent, cuts, -0.22, 0.18) * values
    return jnp.clip(values, min=-bound, max=bound).astype(held_as)


def setup_inputs(seed: int = 0) -> dict:
    key_list = jax.random.split(jax.random.key(seed), 6)
    orbitals = noise(key_list[0], (E, NB, NS), 1.0, 6.0, ((0, 768),))
    rotation = noise(key_list[1], (NS, NS), NS ** -0.5, 0.21875)
    counts = draw_counts(jax.random.fold_in(key_list[5], 71), 0)
    neighbors = draw_neighbors(jax.random.fold_in(key_list[5], 71), 0)
    blocks = noise(key_list[4], (E, 5, NB, NB), (5 * NB) ** -0.5, 0.21875, ((0, 128),))
    return {"orbitals": orbitals, "rotation": rotation, "counts": counts, "neighbors": neighbors, "blocks": blocks}


center_shift = 0.2
half_span = 1.1


def reference(orbitals, rotation, counts, neighbors, blocks):
    total = orbitals.shape[0]
    flat = jnp.dot(orbitals.reshape(total * NB, NS), rotation, preferred_element_type=jnp.float32)
    flat = flat.reshape(total, NB, NS)
    row_mask = (jnp.arange(NB, dtype=jnp.int32)[None, :, None] < counts[:, None, None]).astype(jnp.float32)
    start = (flat * row_mask).astype(jnp.bfloat16)

    def chebyshev(current, previous, factor, with_prev):
        def one_slab(slab):
            lower = (slab * E_LOC).astype(jnp.int32)
            source = lax.dynamic_slice_in_dim(neighbors, lower, E_LOC, 0)
            local_blocks = lax.dynamic_slice_in_dim(blocks, lower, E_LOC, 0).astype(jnp.float32)
            local_mask = lax.dynamic_slice_in_dim(row_mask, lower, E_LOC, 0)
            gathered = current[source].astype(jnp.float32)
            image = jnp.einsum("ekij,ekjs->eis", local_blocks, gathered) * local_mask
            here = lax.dynamic_slice_in_dim(current, lower, E_LOC, 0).astype(jnp.float32)
            value = factor * (image - center_shift * here) / half_span
            if with_prev:
                value = value - lax.dynamic_slice_in_dim(previous, lower, E_LOC, 0).astype(jnp.float32)
            return value.astype(jnp.bfloat16)

        result = lax.map(one_slab, jnp.arange(N_ELEM, dtype=jnp.int32))
        return result.reshape(total, NB, NS)

    previous = start
    current = chebyshev(start, start, 1.0, False)
    for degree in range(DEG - 1):
        following = chebyshev(current, previous, 2.0, True)
        previous = current
        current = following
    return current
```

```python
import functools

import jax
import jax.numpy as jnp
from jax import lax
from jax.experimental import pallas as pl
from jax.experimental.pallas import tpu as pltpu
from jax.sharding import PartitionSpec as P

MESH = pl.DeviceIdType.MESH
DEG = 4
center_shift = 0.2
half_span = 1.1


def kernel(
    n_elem, n_state, counts, neighbors, orbitals, rotation, blocks_hbm, out,
    fields, far_halo, near_halo, last, staged, blocks, blocks_sem,
    a2a_send, a2a_recv, far_send, far_recv, near_send, near_recv, out_send, out_recv, own_sem,
):
    me, spot = lax.axis_index("elem"), lax.axis_index("state")
    core = lax.rem(me, 2)
    high = lax.rem(me // 2, 2)
    elems, reach = last.shape[0], 4
    half = reach // 2
    rows, width = fields.shape[2], fields.shape[3]
    total = n_elem * elems

    def block_at(place):
        return jnp.where(high == 0, place, n_state - 1 - place)

    mine = block_at(spot)
    far = lax.rem(me + jnp.where(core == 0, n_elem - 1, 1), n_elem)
    far_id = (far, n_state - 1 - spot)
    near_id = (me + 1 - 2 * core, spot)

    load = pltpu.make_async_copy(blocks_hbm, blocks, blocks_sem)
    load.start()

    barrier = pltpu.get_barrier_semaphore()
    for step in range(1, n_state):
        pl.semaphore_signal(
            barrier, inc=1, device_id=(me, lax.rem(spot + step, n_state)), device_id_type=MESH
        )
    for device in (far_id, near_id):
        pl.semaphore_signal(barrier, inc=1, device_id=device, device_id_type=MESH)

    row = lax.broadcasted_iota(jnp.int32, (rows, width), 0)
    limits = [counts[2 * spot], counts[2 * spot + 1]]

    def rotated(place):
        columns = pl.ds(pl.multiple_of(block_at(place) * width, width), width)
        result = jnp.dot(
            orbitals[...], rotation[:, columns], preferred_element_type=jnp.float32
        )
        return [
            jnp.where(row < limits[a], result[a * rows:(a + 1) * rows], 0.0).astype(jnp.bfloat16)
            for a in range(2)
        ]

    def a2a_copy(step):
        place = lax.rem(spot + step, n_state)
        return pltpu.make_async_remote_copy(
            src_ref=staged.at[step],
            dst_ref=fields.at[0, pl.ds(reach + 2 * spot, 2)],
            send_sem=a2a_send.at[step],
            recv_sem=a2a_recv.at[spot],
            device_id=(me, place),
            device_id_type=MESH,
        )

    def stage(step):
        pair = rotated(lax.rem(spot + step, n_state))
        for a in range(2):
            staged[step, a] = pair[a]

    stage(1)
    pl.semaphore_wait(barrier, n_state + 1)
    a2a_copy(1).start()

    @pl.loop(2, n_state)
    def _(step):
        stage(step)
        a2a_copy(step).start()

    own = rotated(spot)
    for a in range(2):
        fields[0, reach + 2 * spot + a] = own[a]

    def arrived(pair):
        @pl.when(pair != spot)
        def _():
            pltpu.make_async_remote_copy(
                src_ref=staged.at[0],
                dst_ref=fields.at[0, pl.ds(reach + 2 * pair, 2)],
                send_sem=a2a_send.at[0],
                recv_sem=a2a_recv.at[pair],
                device_id=(me, pair),
                device_id_type=MESH,
            ).wait_recv()

    far_own = jnp.where(core == 0, 0, elems - reach)
    near_own = jnp.where(core == 0, elems - reach, 0)
    far_slot = jnp.where(core == 0, 0, elems + reach)
    near_slot = jnp.where(core == 0, elems + reach, 0)

    def halo(level, side, piece):
        first, landing, device, send, recv = (
            (far_own, far_halo, far_id, far_send, far_recv)
            if side == "far"
            else (near_own, near_halo, near_id, near_send, near_recv)
        )
        return pltpu.make_async_remote_copy(
            src_ref=fields.at[level, pl.ds(reach + first + 2 * piece, 2)],
            dst_ref=landing.at[level, pl.ds(2 * piece, 2)],
            send_sem=send.at[level, piece],
            recv_sem=recv.at[level, piece],
            device_id=device,
            device_id_type=MESH,
        )

    for side, first in (("far", far_own), ("near", near_own)):
        for piece in range(half):
            arrived(first // 2 + piece)
            halo(0, side, piece).start()
    for pair in range(half, elems // 2 - half):
        arrived(pair)
    load.wait()

    start_of_all = me * elems - reach

    def updated(level, e):
        image = jnp.zeros((rows, width), jnp.float32)
        for k in range(5):
            source = neighbors[e, k] - start_of_all
            source = jnp.where(source < 0, source + total, source)
            source = jnp.where(source >= total, source - total, source)
            source = jnp.clip(source, 0, elems + 2 * reach - 1)
            image += jnp.dot(
                blocks[e, k], fields[level - 1, source], preferred_element_type=jnp.float32
            )
        image = jnp.where(row < counts[e], image, 0.0)
        current = fields[level - 1, reach + e].astype(jnp.float32)
        factor = (1.0 if level == 1 else 2.0) / half_span
        value = factor * (image - center_shift * current)
        if level > 1:
            value = value - fields[level - 2, reach + e].astype(jnp.float32)
        return value.astype(jnp.bfloat16)

    def pair_of(level, pair):
        @pl.loop(0, 2)
        def _(a):
            e = 2 * pair + a
            if level < DEG:
                fields[level, reach + e] = updated(level, e)
            else:
                last[e] = updated(level, e)

    def out_copy(pair, source_pair):
        columns = pl.ds(pl.multiple_of(mine * width, width), width)
        return pltpu.make_async_remote_copy(
            src_ref=last.at[pl.ds(2 * pair, 2)],
            dst_ref=out.at[:, :, columns],
            send_sem=out_send.at[pair],
            recv_sem=out_recv.at[source_pair],
            device_id=(me, pair),
            device_id_type=MESH,
        )

    columns_mine = pl.ds(pl.multiple_of(mine * width, width), width)

    def own_copy():
        return pltpu.make_async_copy(
            last.at[pl.ds(2 * spot, 2)], out.at[:, :, columns_mine], own_sem
        )

    def ship(pair):
        @pl.when(pair != spot)
        def _():
            out_copy(pair, spot).start()

        @pl.when(pair == spot)
        def _():
            own_copy().start()

    for level in range(1, DEG + 1):
        for pair in range(half, elems // 2 - half):
            pair_of(level, pair)
            if level == DEG:
                ship(pair)
        for side, first, slot, landing in (
            ("near", near_own, near_slot, near_halo), ("far", far_own, far_slot, far_halo)
        ):
            for piece in range(half):
                halo(level - 1, side, piece).wait_recv()
            fields[level - 1, pl.ds(slot, reach)] = landing[level - 1]
            for piece in range(half):
                pair = first // 2 + piece
                pair_of(level, pair)
                if level < DEG:
                    halo(level, side, piece).start()
                else:
                    ship(pair)

    for place in range(n_state):
        @pl.when(place != spot)
        def _():
            columns = pl.ds(pl.multiple_of(block_at(place) * width, width), width)
            pltpu.make_async_remote_copy(
                src_ref=last.at[pl.ds(0, 2)],
                dst_ref=out.at[:, :, columns],
                send_sem=out_send.at[place],
                recv_sem=out_recv.at[place],
                device_id=(me, place),
                device_id_type=MESH,
            ).wait_recv()
            out_copy(place, spot).wait_send()
    own_copy().wait()
    for step in range(1, n_state):
        a2a_copy(step).wait_send()
    for level in range(DEG):
        for side in ("far", "near"):
            for piece in range(half):
                halo(level, side, piece).wait_send()


def on_device(n_elem, n_state, orbitals, rotation, counts, neighbors, blocks):
    pair, rows, states = orbitals.shape
    elems = counts.shape[0]
    width = states // n_state
    vmem, smem = (pl.BlockSpec(memory_space=s) for s in (pltpu.VMEM, pltpu.SMEM))
    dma = pltpu.SemaphoreType.DMA
    return pl.pallas_call(
        functools.partial(kernel, n_elem, n_state),
        out_shape=jax.ShapeDtypeStruct((pair, rows, states), jnp.bfloat16),
        in_specs=[smem, smem, vmem, vmem, pl.BlockSpec(memory_space=pl.ANY)],
        out_specs=vmem,
        scratch_shapes=[
            pltpu.VMEM((DEG, elems + 8, rows, width), jnp.bfloat16),
            pltpu.VMEM((DEG, 4, rows, width), jnp.bfloat16),
            pltpu.VMEM((DEG, 4, rows, width), jnp.bfloat16),
            pltpu.VMEM((elems, rows, width), jnp.bfloat16),
            pltpu.VMEM((n_state, pair, rows, width), jnp.bfloat16),
            pltpu.VMEM(blocks.shape, jnp.bfloat16),
            dma,
            dma((n_state,)),
            dma((n_state,)),
            dma((DEG, 2)),
            dma((DEG, 2)),
            dma((DEG, 2)),
            dma((DEG, 2)),
            dma((n_state,)),
            dma((n_state,)),
            dma,
        ],
        compiler_params=pltpu.CompilerParams(
            collective_id=0, has_side_effects=True, vmem_limit_bytes=48 * 1024 * 1024
        ),
    )(counts, neighbors, orbitals.reshape(pair * rows, states), rotation, blocks)


def solution(mesh):
    n_elem, n_state = mesh.shape["elem"], mesh.shape["state"]
    in_specs = (
        P(("elem", "state"), None, None),
        P(),
        P("elem"),
        P("elem", None),
        P("elem", None, None, None),
    )
    return jax.shard_map(
        functools.partial(on_device, n_elem, n_state),
        mesh=mesh,
        in_specs=in_specs,
        out_specs=P(("elem", "state"), None, None),
        check_vma=False,
    )
```

```python
import functools

import jax
import jax.numpy as jnp
from jax import lax
from jax.experimental import pallas as pl
from jax.experimental.pallas import tpu as pltpu
from jax.sharding import PartitionSpec as P

MESH = pl.DeviceIdType.MESH
DEG = 4
center_shift = 0.2
half_span = 1.1


def kernel(
    n_elem, n_state, counts_hbm, neighbors_hbm, orbitals_hbm, rotation_hbm, blocks_hbm, out,
    counts, neighbors, orbitals, rotation, load_sem, fields, far_out, far_halo, near_halo, last,
    staged, landed, homed, blocks, scratch, own_counts, far_counts, count_send, count_recv,
    a2a_send, a2a_recv, far_send, far_recv, near_send, near_recv, out_send, out_recv,
):
    me, spot = lax.axis_index("elem"), lax.axis_index("state")
    core = lax.rem(me, 2)
    high = lax.rem(me // 2, 2)
    elems, reach = counts.shape[0], 4
    half = reach // 2
    rows, width = fields.shape[2], fields.shape[3]
    total = n_elem * elems

    def block_at(place):
        return jnp.where(high == 0, place, n_state - 1 - place)

    mine = block_at(spot)
    far = lax.rem(me + jnp.where(core == 0, n_elem - 1, 1), n_elem)
    far_id = (far, n_state - 1 - spot)
    near_id = (me + 1 - 2 * core, spot)

    loads = [
        pltpu.make_async_copy(source, target, load_sem.at[i])
        for i, (source, target) in enumerate([
            (counts_hbm, counts), (orbitals_hbm, orbitals), (rotation_hbm, rotation),
            (neighbors_hbm, neighbors), (blocks_hbm, blocks),
        ])
    ]
    for load in loads:
        load.start()

    barrier = pltpu.get_barrier_semaphore()
    for step in range(1, n_state):
        pl.semaphore_signal(
            barrier, inc=1, device_id=(me, lax.rem(spot + step, n_state)), device_id_type=MESH
        )
    for device in (far_id, near_id):
        pl.semaphore_signal(barrier, inc=1, device_id=device, device_id_type=MESH)

    for load in loads[:3]:
        load.wait()
    row = lax.broadcasted_iota(jnp.int32, (rows, width), 0)
    main = 128
    tail = rows - main
    tail_row = row[:tail]
    flip = (
        lax.broadcasted_iota(jnp.int32, (tail, tail), 0)
        + lax.broadcasted_iota(jnp.int32, (tail, tail), 1)
        == tail - 1
    ).astype(jnp.bfloat16)

    def flipped(part):
        return jnp.dot(flip, part, preferred_element_type=jnp.float32).astype(jnp.bfloat16)

    def pack(target, first, second):
        target[0:main] = first[:main]
        target[main:2 * main] = second[:main]
        target[2 * main:] = first[main:] + flipped(second[main:])

    def unpack(source, limit_first, limit_second):
        shared = source[2 * main:]
        zero = jnp.zeros_like(shared)
        return (
            jnp.where(tail_row < limit_first - main, shared, zero),
            jnp.where(tail_row < limit_second - main, flipped(shared), zero),
        )

    def a2a_copy(place):
        return pltpu.make_async_remote_copy(
            src_ref=staged.at[place],
            dst_ref=landed.at[spot],
            send_sem=a2a_send.at[place],
            recv_sem=a2a_recv.at[spot],
            device_id=(me, place),
            device_id_type=MESH,
        )

    def place_at(step):
        return jnp.where(lax.rem(step, 2) == 0, step // 2, n_state - 1 - step // 2)

    limits = [counts[2 * spot], counts[2 * spot + 1]]

    def stage(step):
        place = place_at(step)
        columns = pl.ds(pl.multiple_of(block_at(place) * width, width), width)
        result = jnp.dot(
            orbitals[...], rotation[:, columns], preferred_element_type=jnp.float32
        )
        first, second = [
            jnp.where(row < limits[a], result[a * rows:(a + 1) * rows], 0.0).astype(jnp.bfloat16)
            for a in range(2)
        ]
        pack(staged.at[place], first, second)

    def send(step):
        place = place_at(step)

        @pl.when(place != spot)
        def _():
            a2a_copy(place).start()

    far_own = jnp.where(core == 0, 0, elems - reach)
    for j in range(reach):
        own_counts[j] = jnp.full((8, width), counts[far_own + j], jnp.int32)
    count_copy = pltpu.make_async_remote_copy(
        src_ref=own_counts,
        dst_ref=far_counts,
        send_sem=count_send,
        recv_sem=count_recv,
        device_id=far_id,
        device_id_type=MESH,
    )
    stage(0)
    pl.semaphore_wait(barrier, n_state + 1)
    send(0)
    count_copy.start()

    @pl.loop(1, n_state)
    def _(step):
        stage(step)
        send(step)

    def arrived(pair):
        @pl.when(pair != spot)
        def _():
            pltpu.make_async_remote_copy(
                src_ref=staged.at[0],
                dst_ref=landed.at[pair],
                send_sem=a2a_send.at[0],
                recv_sem=a2a_recv.at[pair],
                device_id=(me, pair),
                device_id_type=MESH,
            ).wait_recv()

        @pl.when(pair == spot)
        def _():
            landed[pair] = staged[pair]

    def settle(pair):
        fields_pair(landed.at[pair], 0, reach + 2 * pair, counts[2 * pair], counts[2 * pair + 1])

    def fields_pair(source, level, slot, limit_first, limit_second):
        tails = unpack(source, limit_first, limit_second)
        for a in range(2):
            fields[level, slot + a, 0:main] = source[a * main:(a + 1) * main]
            fields[level, slot + a, main:] = tails[a]

    near_own = jnp.where(core == 0, elems - reach, 0)
    far_slot = jnp.where(core == 0, 0, elems + reach)
    near_slot = jnp.where(core == 0, elems + reach, 0)

    def far_copy(level, piece):
        return pltpu.make_async_remote_copy(
            src_ref=landed.at[far_own // 2 + piece] if level == 0 else far_out.at[level, piece],
            dst_ref=far_halo.at[level, piece],
            send_sem=far_send.at[level, piece],
            recv_sem=far_recv.at[level, piece],
            device_id=far_id,
            device_id_type=MESH,
        )

    def near_copy(level, piece):
        return pltpu.make_async_remote_copy(
            src_ref=fields.at[level, pl.ds(reach + near_own + 2 * piece, 2)],
            dst_ref=near_halo.at[level, pl.ds(2 * piece, 2)],
            send_sem=near_send.at[level, piece],
            recv_sem=near_recv.at[level, piece],
            device_id=near_id,
            device_id_type=MESH,
        )

    for piece in range(half):
        arrived(far_own // 2 + piece)
        far_copy(0, piece).start()
    for piece in range(half):
        pair = near_own // 2 + piece
        arrived(pair)
        settle(pair)
        near_copy(0, piece).start()
    for piece in range(half):
        settle(far_own // 2 + piece)
    for pair in range(half, elems // 2 - half):
        arrived(pair)
        settle(pair)
    count_copy.wait()
    for load in loads[3:]:
        load.wait()

    start_of_all = me * elems - reach

    def updated(level, e):
        image = jnp.zeros((rows, width), jnp.float32)
        for k in range(5):
            source = neighbors[k, e] - start_of_all
            source = jnp.where(source < 0, source + total, source)
            source = jnp.where(source >= total, source - total, source)
            source = jnp.clip(source, 0, elems + 2 * reach - 1)
            image += jnp.dot(
                blocks[e, k], fields[level - 1, source], preferred_element_type=jnp.float32
            )
        image = jnp.where(row < counts[e], image, 0.0)
        current = fields[level - 1, reach + e].astype(jnp.float32)
        factor = (1.0 if level == 1 else 2.0) / half_span
        value = factor * (image - center_shift * current)
        if level > 1:
            value = value - fields[level - 2, reach + e].astype(jnp.float32)
        return value.astype(jnp.bfloat16)

    def pair_of(level, pair):
        if level < DEG:
            @pl.loop(0, 2)
            def _(a):
                e = 2 * pair + a
                fields[level, reach + e] = updated(level, e)
        else:
            @pl.loop(0, 2)
            def _(a):
                scratch[a] = updated(level, 2 * pair + a)

            pack(last.at[pair], scratch[0], scratch[1])

    def out_copy(pair):
        return pltpu.make_async_remote_copy(
            src_ref=last.at[pair],
            dst_ref=homed.at[spot],
            send_sem=out_send.at[pair],
            recv_sem=out_recv.at[spot],
            device_id=(me, pair),
            device_id_type=MESH,
        )

    def ship(pair):
        @pl.when(pair != spot)
        def _():
            out_copy(pair).start()

    for level in range(1, DEG + 1):
        for pair in range(half, elems // 2 - half):
            pair_of(level, pair)
            if level == DEG:
                ship(pair)
        for piece in range(half):
            near_copy(level - 1, piece).wait_recv()
        fields[level - 1, pl.ds(near_slot, reach)] = near_halo[level - 1]
        for piece in range(half):
            pair = near_own // 2 + piece
            pair_of(level, pair)
            if level < DEG:
                near_copy(level, piece).start()
            else:
                ship(pair)
        for piece in range(half):
            far_copy(level - 1, piece).wait_recv()
            fields_pair(
                far_halo.at[level - 1, piece],
                level - 1,
                far_slot + 2 * piece,
                far_counts[2 * piece, 0:1],
                far_counts[2 * piece + 1, 0:1],
            )
        for piece in range(half):
            pair = far_own // 2 + piece
            pair_of(level, pair)
            if level < DEG:
                slot = reach + 2 * pair
                pack(far_out.at[level, piece], fields[level, slot], fields[level, slot + 1])
                far_copy(level, piece).start()
            else:
                ship(pair)

    def deliver(source, place):
        columns = pl.ds(pl.multiple_of(block_at(place) * width, width), width)
        tails = unpack(source, limits[0], limits[1])
        for a in range(2):
            out[a, 0:main, columns] = source[a * main:(a + 1) * main]
            out[a, main:, columns] = tails[a]

    deliver(last.at[spot], spot)
    for step in range(1, n_state):
        place = lax.rem(spot + step, n_state)
        pltpu.make_async_remote_copy(
            src_ref=last.at[0],
            dst_ref=homed.at[place],
            send_sem=out_send.at[place],
            recv_sem=out_recv.at[place],
            device_id=(me, place),
            device_id_type=MESH,
        ).wait_recv()
        deliver(homed.at[place], place)
        out_copy(place).wait_send()
        a2a_copy(place).wait_send()
    for level in range(DEG):
        for piece in range(half):
            far_copy(level, piece).wait_send()
            near_copy(level, piece).wait_send()


def on_device(n_elem, n_state, orbitals, rotation, counts, neighbors, blocks):
    pair, rows, states = orbitals.shape
    elems = counts.shape[0]
    width = states // n_state
    packed = 2 * rows - 32
    dma = pltpu.SemaphoreType.DMA
    return pl.pallas_call(
        functools.partial(kernel, n_elem, n_state),
        out_shape=jax.ShapeDtypeStruct((pair, rows, states), jnp.bfloat16),
        in_specs=[pl.BlockSpec(memory_space=pltpu.HBM)] * 5,
        out_specs=pl.BlockSpec(memory_space=pltpu.VMEM),
        scratch_shapes=[
            pltpu.SMEM(counts.shape, jnp.int32),
            pltpu.SMEM(neighbors.shape[::-1], jnp.int32),
            pltpu.VMEM((pair * rows, states), jnp.bfloat16),
            pltpu.VMEM(rotation.shape, jnp.bfloat16),
            dma((5,)),
            pltpu.VMEM((DEG, elems + 8, rows, width), jnp.bfloat16),
            pltpu.VMEM((DEG, 2, packed, width), jnp.bfloat16),
            pltpu.VMEM((DEG, 2, packed, width), jnp.bfloat16),
            pltpu.VMEM((DEG, 4, rows, width), jnp.bfloat16),
            pltpu.VMEM((n_state, packed, width), jnp.bfloat16),
            pltpu.VMEM((n_state, packed, width), jnp.bfloat16),
            pltpu.VMEM((n_state, packed, width), jnp.bfloat16),
            pltpu.VMEM((n_state, packed, width), jnp.bfloat16),
            pltpu.VMEM(blocks.shape, jnp.bfloat16),
            pltpu.VMEM((2, rows, width), jnp.bfloat16),
            pltpu.VMEM((4, 8, width), jnp.int32),
            pltpu.VMEM((4, 8, width), jnp.int32),
            dma,
            dma,
            dma((n_state,)),
            dma((n_state,)),
            dma((DEG, 2)),
            dma((DEG, 2)),
            dma((DEG, 2)),
            dma((DEG, 2)),
            dma((n_state,)),
            dma((n_state,)),
        ],
        compiler_params=pltpu.CompilerParams(
            collective_id=0, has_side_effects=True, vmem_limit_bytes=66000000
        ),
    )(counts, neighbors.T, orbitals.reshape(pair * rows, states), rotation, blocks)


def solution(mesh):
    n_elem, n_state = mesh.shape["elem"], mesh.shape["state"]
    in_specs = (
        P(("elem", "state"), None, None),
        P(),
        P("elem"),
        P("elem", None),
        P("elem", None, None, None),
    )
    return jax.shard_map(
        functools.partial(on_device, n_elem, n_state),
        mesh=mesh,
        in_specs=in_specs,
        out_specs=P(("elem", "state"), None, None),
        check_vma=False,
    )
```

```python
import functools

import jax
import jax.numpy as jnp
from jax import lax
from jax.experimental import pallas as pl
from jax.experimental.pallas import tpu as pltpu
from jax.sharding import PartitionSpec as P

MESH = pl.DeviceIdType.MESH
DEG = 4
center_shift = 0.2
half_span = 1.1


def kernel(
    n_elem, n_state, counts_hbm, neighbors_hbm, orbitals_hbm, rotation_hbm, blocks_hbm, out,
    counts, neighbors, orbitals, rotation, load_sem, column_sem, fields, far_out, far_halo, near_halo, last,
    staged, landed, homed, blocks, scratch, own_counts, far_counts, count_send, count_recv,
    a2a_send, a2a_recv, far_send, far_recv, near_send, near_recv, out_send, out_recv,
):
    me, spot = lax.axis_index("elem"), lax.axis_index("state")
    core = lax.rem(me, 2)
    high = lax.rem(me // 2, 2)
    elems, reach = counts.shape[0], 4
    half = reach // 2
    rows, width = fields.shape[2], fields.shape[3]
    total = n_elem * elems

    def block_at(place):
        return jnp.where(high == 0, place, n_state - 1 - place)

    mine = block_at(spot)
    far = lax.rem(me + jnp.where(core == 0, n_elem - 1, 1), n_elem)
    far_id = (far, n_state - 1 - spot)
    near_id = (me + 1 - 2 * core, spot)

    def column_load(place):
        columns = pl.ds(pl.multiple_of(block_at(place) * width, width), width)
        return pltpu.make_async_copy(
            rotation_hbm.at[:, columns], rotation.at[:, columns], column_sem.at[place]
        )

    furthest = jnp.where(spot < n_state // 2, n_state - 1, 0)
    loads = [
        pltpu.make_async_copy(source, target, load_sem.at[i])
        for i, (source, target) in enumerate([
            (counts_hbm, counts), (orbitals_hbm, orbitals),
            (neighbors_hbm, neighbors), (blocks_hbm, blocks),
        ])
    ]
    column_load(furthest).start()
    for load in loads[:2]:
        load.start()
    for step in range(1, n_state):
        column_load(lax.rem(furthest + step, n_state)).start()

    barrier = pltpu.get_barrier_semaphore()
    for step in range(1, n_state):
        pl.semaphore_signal(
            barrier, inc=1, device_id=(me, lax.rem(spot + step, n_state)), device_id_type=MESH
        )
    for device in (far_id, near_id):
        pl.semaphore_signal(barrier, inc=1, device_id=device, device_id_type=MESH)

    for load in loads[:2]:
        load.wait()
    row = lax.broadcasted_iota(jnp.int32, (rows, width), 0)
    main = 128
    tail = rows - main
    tail_row = row[:tail]
    flip = (
        lax.broadcasted_iota(jnp.int32, (tail, tail), 0)
        + lax.broadcasted_iota(jnp.int32, (tail, tail), 1)
        == tail - 1
    ).astype(jnp.bfloat16)

    def flipped(part):
        return jnp.dot(flip, part, preferred_element_type=jnp.float32).astype(jnp.bfloat16)

    def pack(target, first, second):
        target[0:main] = first[:main]
        target[main:2 * main] = second[:main]
        target[2 * main:] = first[main:] + flipped(second[main:])

    def unpack(source, limit_first, limit_second):
        shared = source[2 * main:]
        zero = jnp.zeros_like(shared)
        return (
            jnp.where(tail_row < limit_first - main, shared, zero),
            jnp.where(tail_row < limit_second - main, flipped(shared), zero),
        )

    def a2a_copy(place):
        return pltpu.make_async_remote_copy(
            src_ref=staged.at[place],
            dst_ref=landed.at[spot],
            send_sem=a2a_send.at[place],
            recv_sem=a2a_recv.at[spot],
            device_id=(me, place),
            device_id_type=MESH,
        )

    limits = [counts[2 * spot], counts[2 * spot + 1]]

    def stage(place):
        columns = pl.ds(pl.multiple_of(block_at(place) * width, width), width)
        column_load(place).wait()
        result = jnp.dot(
            orbitals[...], rotation[:, columns], preferred_element_type=jnp.float32
        )
        first, second = [
            jnp.where(row < limits[a], result[a * rows:(a + 1) * rows], 0.0).astype(jnp.bfloat16)
            for a in range(2)
        ]
        pack(staged.at[place], first, second)

    far_own = jnp.where(core == 0, 0, elems - reach)
    for j in range(reach):
        own_counts[j] = jnp.full((8, width), counts[far_own + j], jnp.int32)
    count_copy = pltpu.make_async_remote_copy(
        src_ref=own_counts,
        dst_ref=far_counts,
        send_sem=count_send,
        recv_sem=count_recv,
        device_id=far_id,
        device_id_type=MESH,
    )
    stage(furthest)
    for load in loads[2:]:
        load.start()
    pl.semaphore_wait(barrier, n_state + 1)
    a2a_copy(furthest).start()
    count_copy.start()

    @pl.loop(1, 2 * n_state - 2)
    def _(step):
        distance = n_state - 1 - step // 2
        side = jnp.where(spot < n_state // 2, 1, -1) * (1 - 2 * lax.rem(step, 2))
        place = spot + side * distance

        @pl.when((place >= 0) & (place < n_state) & (place != furthest))
        def _():
            stage(place)
            a2a_copy(place).start()

    stage(spot)

    def arrived(pair):
        @pl.when(pair != spot)
        def _():
            pltpu.make_async_remote_copy(
                src_ref=staged.at[0],
                dst_ref=landed.at[pair],
                send_sem=a2a_send.at[0],
                recv_sem=a2a_recv.at[pair],
                device_id=(me, pair),
                device_id_type=MESH,
            ).wait_recv()

        @pl.when(pair == spot)
        def _():
            landed[pair] = staged[pair]

    def settle(pair):
        fields_pair(landed.at[pair], 0, reach + 2 * pair, counts[2 * pair], counts[2 * pair + 1])

    def fields_pair(source, level, slot, limit_first, limit_second):
        tails = unpack(source, limit_first, limit_second)
        for a in range(2):
            fields[level, slot + a, 0:main] = source[a * main:(a + 1) * main]
            fields[level, slot + a, main:] = tails[a]

    near_own = jnp.where(core == 0, elems - reach, 0)
    far_slot = jnp.where(core == 0, 0, elems + reach)
    near_slot = jnp.where(core == 0, elems + reach, 0)

    def far_copy(level, piece):
        return pltpu.make_async_remote_copy(
            src_ref=landed.at[far_own // 2 + piece] if level == 0 else far_out.at[level, piece],
            dst_ref=far_halo.at[level, piece],
            send_sem=far_send.at[level, piece],
            recv_sem=far_recv.at[level, piece],
            device_id=far_id,
            device_id_type=MESH,
        )

    def near_copy(level, piece):
        return pltpu.make_async_remote_copy(
            src_ref=fields.at[level, pl.ds(reach + near_own + 2 * piece, 2)],
            dst_ref=near_halo.at[level, pl.ds(2 * piece, 2)],
            send_sem=near_send.at[level, piece],
            recv_sem=near_recv.at[level, piece],
            device_id=near_id,
            device_id_type=MESH,
        )

    for piece in range(half):
        arrived(far_own // 2 + piece)
        far_copy(0, piece).start()
    for piece in range(half):
        pair = near_own // 2 + piece
        arrived(pair)
        settle(pair)
        near_copy(0, piece).start()
    for piece in range(half):
        settle(far_own // 2 + piece)
    for pair in range(half, elems // 2 - half):
        arrived(pair)
        settle(pair)
    count_copy.wait()
    for load in loads[2:]:
        load.wait()

    start_of_all = me * elems - reach

    def updated(level, e):
        image = jnp.zeros((rows, width), jnp.float32)
        for k in range(5):
            source = neighbors[k, e] - start_of_all
            source = jnp.where(source < 0, source + total, source)
            source = jnp.where(source >= total, source - total, source)
            source = jnp.clip(source, 0, elems + 2 * reach - 1)
            image += jnp.dot(
                blocks[e, k], fields[level - 1, source], preferred_element_type=jnp.float32
            )
        image = jnp.where(row < counts[e], image, 0.0)
        current = fields[level - 1, reach + e].astype(jnp.float32)
        factor = (1.0 if level == 1 else 2.0) / half_span
        value = factor * (image - center_shift * current)
        if level > 1:
            value = value - fields[level - 2, reach + e].astype(jnp.float32)
        return value.astype(jnp.bfloat16)

    def pair_of(level, pair):
        if level < DEG:
            @pl.loop(0, 2)
            def _(a):
                e = 2 * pair + a
                fields[level, reach + e] = updated(level, e)
        else:
            @pl.loop(0, 2)
            def _(a):
                scratch[a] = updated(level, 2 * pair + a)

            pack(last.at[pair], scratch[0], scratch[1])

    def out_copy(pair):
        return pltpu.make_async_remote_copy(
            src_ref=last.at[pair],
            dst_ref=homed.at[spot],
            send_sem=out_send.at[pair],
            recv_sem=out_recv.at[spot],
            device_id=(me, pair),
            device_id_type=MESH,
        )

    def ship(pair):
        @pl.when(pair != spot)
        def _():
            out_copy(pair).start()

    for level in range(1, DEG + 1):
        for pair in range(half, elems // 2 - half):
            pair_of(level, pair)
            if level == DEG:
                ship(pair)
        for piece in range(half):
            near_copy(level - 1, piece).wait_recv()
        fields[level - 1, pl.ds(near_slot, reach)] = near_halo[level - 1]
        for piece in range(half):
            pair = near_own // 2 + piece
            pair_of(level, pair)
            if level < DEG:
                near_copy(level, piece).start()
            else:
                ship(pair)
        for piece in range(half):
            far_copy(level - 1, piece).wait_recv()
            fields_pair(
                far_halo.at[level - 1, piece],
                level - 1,
                far_slot + 2 * piece,
                far_counts[2 * piece, 0:1],
                far_counts[2 * piece + 1, 0:1],
            )
        for piece in range(half):
            pair = far_own // 2 + piece
            pair_of(level, pair)
            if level < DEG:
                slot = reach + 2 * pair
                pack(far_out.at[level, piece], fields[level, slot], fields[level, slot + 1])
                far_copy(level, piece).start()
            else:
                ship(pair)

    def deliver(source, place):
        columns = pl.ds(pl.multiple_of(block_at(place) * width, width), width)
        tails = unpack(source, limits[0], limits[1])
        for a in range(2):
            out[a, 0:main, columns] = source[a * main:(a + 1) * main]
            out[a, main:, columns] = tails[a]

    deliver(last.at[spot], spot)
    for step in range(1, n_state):
        place = lax.rem(spot + step, n_state)
        pltpu.make_async_remote_copy(
            src_ref=last.at[0],
            dst_ref=homed.at[place],
            send_sem=out_send.at[place],
            recv_sem=out_recv.at[place],
            device_id=(me, place),
            device_id_type=MESH,
        ).wait_recv()
        deliver(homed.at[place], place)
        out_copy(place).wait_send()
        a2a_copy(place).wait_send()
    for level in range(DEG):
        for piece in range(half):
            far_copy(level, piece).wait_send()
            near_copy(level, piece).wait_send()


def on_device(n_elem, n_state, orbitals, rotation, counts, neighbors, blocks):
    pair, rows, states = orbitals.shape
    elems = counts.shape[0]
    width = states // n_state
    packed = 2 * rows - 32
    dma = pltpu.SemaphoreType.DMA
    return pl.pallas_call(
        functools.partial(kernel, n_elem, n_state),
        out_shape=jax.ShapeDtypeStruct((pair, rows, states), jnp.bfloat16),
        in_specs=[pl.BlockSpec(memory_space=pltpu.HBM)] * 5,
        out_specs=pl.BlockSpec(memory_space=pltpu.VMEM),
        scratch_shapes=[
            pltpu.SMEM(counts.shape, jnp.int32),
            pltpu.SMEM(neighbors.shape[::-1], jnp.int32),
            pltpu.VMEM((pair * rows, states), jnp.bfloat16),
            pltpu.VMEM(rotation.shape, jnp.bfloat16),
            dma((4,)),
            dma((n_state,)),
            pltpu.VMEM((DEG, elems + 8, rows, width), jnp.bfloat16),
            pltpu.VMEM((DEG, 2, packed, width), jnp.bfloat16),
            pltpu.VMEM((DEG, 2, packed, width), jnp.bfloat16),
            pltpu.VMEM((DEG, 4, rows, width), jnp.bfloat16),
            pltpu.VMEM((n_state, packed, width), jnp.bfloat16),
            pltpu.VMEM((n_state, packed, width), jnp.bfloat16),
            pltpu.VMEM((n_state, packed, width), jnp.bfloat16),
            pltpu.VMEM((n_state, packed, width), jnp.bfloat16),
            pltpu.VMEM(blocks.shape, jnp.bfloat16),
            pltpu.VMEM((2, rows, width), jnp.bfloat16),
            pltpu.VMEM((4, 8, width), jnp.int32),
            pltpu.VMEM((4, 8, width), jnp.int32),
            dma,
            dma,
            dma((n_state,)),
            dma((n_state,)),
            dma((DEG, 2)),
            dma((DEG, 2)),
            dma((DEG, 2)),
            dma((DEG, 2)),
            dma((n_state,)),
            dma((n_state,)),
        ],
        compiler_params=pltpu.CompilerParams(
            collective_id=0, has_side_effects=True, vmem_limit_bytes=48 * 1024 * 1024
        ),
    )(*[
        pltpu.with_memory_space_constraint(x, pltpu.HBM)
        for x in (counts, neighbors.T, orbitals.reshape(pair * rows, states), rotation, blocks)
    ])


def solution(mesh):
    n_elem, n_state = mesh.shape["elem"], mesh.shape["state"]
    in_specs = (
        P(("elem", "state"), None, None),
        P(),
        P("elem"),
        P("elem", None),
        P("elem", None, None, None),
    )
    return jax.shard_map(
        functools.partial(on_device, n_elem, n_state),
        mesh=mesh,
        in_specs=in_specs,
        out_specs=P(("elem", "state"), None, None),
        check_vma=False,
    )
```

```python
import functools

import jax
import jax.numpy as jnp
from jax import lax
from jax.experimental import pallas as pl
from jax.experimental.pallas import tpu as pltpu
from jax.sharding import PartitionSpec as P

MESH = pl.DeviceIdType.MESH
DEG = 4
center_shift = 0.2
half_span = 1.1


def kernel(
    n_elem, n_state, counts_hbm, neighbors_hbm, orbitals_hbm, rotation_hbm, blocks_hbm, out,
    counts, neighbors, orbitals, rotation, load_sem, column_sem, fields, far_out, far_halo, near_halo, last,
    staged, landed, homed, blocks, scratch, own_counts, far_counts, count_send, count_recv,
    a2a_send, a2a_recv, far_send, far_recv, near_send, near_recv, out_send, out_recv,
):
    me, spot = lax.axis_index("elem"), lax.axis_index("state")
    core = lax.rem(me, 2)
    high = lax.rem(me // 2, 2)
    elems, reach = counts.shape[0], 4
    half = reach // 2
    rows, width = fields.shape[2], fields.shape[3]
    total = n_elem * elems

    def block_at(place):
        return jnp.where(high == 0, place, n_state - 1 - place)

    mine = block_at(spot)
    far = lax.rem(me + jnp.where(core == 0, n_elem - 1, 1), n_elem)
    far_id = (far, n_state - 1 - spot)
    near_id = (me + 1 - 2 * core, spot)

    def column_load(place):
        columns = pl.ds(pl.multiple_of(block_at(place) * width, width), width)
        return pltpu.make_async_copy(
            rotation_hbm.at[:, columns], rotation.at[:, columns], column_sem.at[place]
        )

    furthest = jnp.where(spot < n_state // 2, n_state - 1, 0)
    loads = [
        pltpu.make_async_copy(source, target, load_sem.at[i])
        for i, (source, target) in enumerate([
            (counts_hbm, counts), (orbitals_hbm, orbitals),
            (neighbors_hbm, neighbors), (blocks_hbm, blocks),
        ])
    ]
    column_load(furthest).start()
    for load in loads[:2]:
        load.start()
    for step in range(1, n_state):
        column_load(lax.rem(furthest + step, n_state)).start()

    barrier = pltpu.get_barrier_semaphore()
    for step in range(1, n_state):
        pl.semaphore_signal(
            barrier, inc=1, device_id=(me, lax.rem(spot + step, n_state)), device_id_type=MESH
        )
    for device in (far_id, near_id):
        pl.semaphore_signal(barrier, inc=1, device_id=device, device_id_type=MESH)

    for load in loads[:2]:
        load.wait()
    row = lax.broadcasted_iota(jnp.int32, (rows, width), 0)
    main = 128
    tail = rows - main
    tail_row = row[:tail]
    flip = (
        lax.broadcasted_iota(jnp.int32, (tail, tail), 0)
        + lax.broadcasted_iota(jnp.int32, (tail, tail), 1)
        == tail - 1
    ).astype(jnp.bfloat16)

    def flipped(part):
        return jnp.dot(flip, part, preferred_element_type=jnp.float32).astype(jnp.bfloat16)

    def pack(target, first, second):
        target[0:main] = first[:main]
        target[main:2 * main] = second[:main]
        target[2 * main:] = first[main:] + flipped(second[main:])

    def unpack(source, limit_first, limit_second):
        shared = source[2 * main:]
        zero = jnp.zeros_like(shared)
        return (
            jnp.where(tail_row < limit_first - main, shared, zero),
            jnp.where(tail_row < limit_second - main, flipped(shared), zero),
        )

    def a2a_copy(place):
        return pltpu.make_async_remote_copy(
            src_ref=staged.at[place],
            dst_ref=landed.at[spot],
            send_sem=a2a_send.at[place],
            recv_sem=a2a_recv.at[spot],
            device_id=(me, place),
            device_id_type=MESH,
        )

    limits = [counts[2 * spot], counts[2 * spot + 1]]

    def stage(place):
        columns = pl.ds(pl.multiple_of(block_at(place) * width, width), width)
        column_load(place).wait()
        result = jnp.dot(
            orbitals[...], rotation[:, columns], preferred_element_type=jnp.float32
        )
        first, second = [
            jnp.where(row < limits[a], result[a * rows:(a + 1) * rows], 0.0).astype(jnp.bfloat16)
            for a in range(2)
        ]
        pack(staged.at[place], first, second)

    far_own = jnp.where(core == 0, 0, elems - reach)
    for j in range(reach):
        own_counts[j] = jnp.full((8, width), counts[far_own + j], jnp.int32)
    count_copy = pltpu.make_async_remote_copy(
        src_ref=own_counts,
        dst_ref=far_counts,
        send_sem=count_send,
        recv_sem=count_recv,
        device_id=far_id,
        device_id_type=MESH,
    )
    stage(furthest)
    for load in loads[2:]:
        load.start()
    pl.semaphore_wait(barrier, n_state + 1)
    a2a_copy(furthest).start()
    count_copy.start()

    @pl.loop(1, 2 * n_state - 2)
    def _(step):
        distance = n_state - 1 - step // 2
        side = jnp.where(spot < n_state // 2, 1, -1) * (1 - 2 * lax.rem(step, 2))
        place = spot + side * distance

        @pl.when((place >= 0) & (place < n_state) & (place != furthest))
        def _():
            stage(place)
            a2a_copy(place).start()

    stage(spot)

    def arrived(pair):
        @pl.when(pair != spot)
        def _():
            pltpu.make_async_remote_copy(
                src_ref=staged.at[0],
                dst_ref=landed.at[pair],
                send_sem=a2a_send.at[0],
                recv_sem=a2a_recv.at[pair],
                device_id=(me, pair),
                device_id_type=MESH,
            ).wait_recv()

        @pl.when(pair == spot)
        def _():
            landed[pair] = staged[pair]

    def settle(pair):
        fields_pair(landed.at[pair], 0, reach + 2 * pair, counts[2 * pair], counts[2 * pair + 1])

    def fields_pair(source, level, slot, limit_first, limit_second):
        tails = unpack(source, limit_first, limit_second)
        for a in range(2):
            fields[level, slot + a, 0:main] = source[a * main:(a + 1) * main]
            fields[level, slot + a, main:] = tails[a]

    near_own = jnp.where(core == 0, elems - reach, 0)
    far_slot = jnp.where(core == 0, 0, elems + reach)
    near_slot = jnp.where(core == 0, elems + reach, 0)

    def far_copy(level, piece):
        return pltpu.make_async_remote_copy(
            src_ref=landed.at[far_own // 2 + piece] if level == 0 else far_out.at[level, piece],
            dst_ref=far_halo.at[level, piece],
            send_sem=far_send.at[level, piece],
            recv_sem=far_recv.at[level, piece],
            device_id=far_id,
            device_id_type=MESH,
        )

    def near_copy(level, piece):
        return pltpu.make_async_remote_copy(
            src_ref=fields.at[level, pl.ds(reach + near_own + 2 * piece, 2)],
            dst_ref=near_halo.at[level, pl.ds(2 * piece, 2)],
            send_sem=near_send.at[level, piece],
            recv_sem=near_recv.at[level, piece],
            device_id=near_id,
            device_id_type=MESH,
        )

    outer, inner = core, 1 - core
    for piece in (inner, outer):
        arrived(far_own // 2 + piece)
        far_copy(0, piece).start()
    for piece in range(half):
        pair = near_own // 2 + piece
        arrived(pair)
        settle(pair)
        near_copy(0, piece).start()
    for piece in range(half):
        settle(far_own // 2 + piece)
    for pair in range(half, elems // 2 - half):
        arrived(pair)
        settle(pair)
    count_copy.wait()
    for load in loads[2:]:
        load.wait()

    start_of_all = me * elems - reach

    def updated(level, e):
        image = jnp.zeros((rows, width), jnp.float32)
        for k in range(5):
            source = neighbors[k, e] - start_of_all
            source = jnp.where(source < 0, source + total, source)
            source = jnp.where(source >= total, source - total, source)
            source = jnp.clip(source, 0, elems + 2 * reach - 1)
            image += jnp.dot(
                blocks[e, k], fields[level - 1, source], preferred_element_type=jnp.float32
            )
        image = jnp.where(row < counts[e], image, 0.0)
        current = fields[level - 1, reach + e].astype(jnp.float32)
        factor = (1.0 if level == 1 else 2.0) / half_span
        value = factor * (image - center_shift * current)
        if level > 1:
            value = value - fields[level - 2, reach + e].astype(jnp.float32)
        return value.astype(jnp.bfloat16)

    def pair_of(level, pair):
        if level < DEG:
            @pl.loop(0, 2)
            def _(a):
                e = 2 * pair + a
                fields[level, reach + e] = updated(level, e)
        else:
            @pl.loop(0, 2)
            def _(a):
                scratch[a] = updated(level, 2 * pair + a)

            pack(last.at[pair], scratch[0], scratch[1])

    def out_copy(pair):
        return pltpu.make_async_remote_copy(
            src_ref=last.at[pair],
            dst_ref=homed.at[spot],
            send_sem=out_send.at[pair],
            recv_sem=out_recv.at[spot],
            device_id=(me, pair),
            device_id_type=MESH,
        )

    def ship(pair):
        @pl.when(pair != spot)
        def _():
            out_copy(pair).start()

    def receive(level, piece):
        far_copy(level, piece).wait_recv()
        fields_pair(
            far_halo.at[level, piece],
            level,
            far_slot + 2 * piece,
            far_counts[2 * piece, 0:1],
            far_counts[2 * piece + 1, 0:1],
        )

    def produce(level, piece):
        pair = far_own // 2 + piece
        pair_of(level, pair)
        if level < DEG:
            slot = reach + 2 * pair
            pack(far_out.at[level, piece], fields[level, slot], fields[level, slot + 1])
            far_copy(level, piece).start()
        else:
            ship(pair)

    for level in range(1, DEG + 1):
        for pair in range(half, elems // 2 - half):
            pair_of(level, pair)
            if level == DEG:
                ship(pair)
        for piece in range(half):
            near_copy(level - 1, piece).wait_recv()
        fields[level - 1, pl.ds(near_slot, reach)] = near_halo[level - 1]
        for piece in range(half):
            pair = near_own // 2 + piece
            pair_of(level, pair)
            if level < DEG:
                near_copy(level, piece).start()
            else:
                ship(pair)
        if level % 2 == 0:
            receive(level - 1, inner)
            produce(level, inner)
            receive(level - 1, outer)
            produce(level, outer)
        else:
            receive(level - 1, outer)
            receive(level - 1, inner)
            produce(level, outer)
            produce(level, inner)

    def deliver(source, place):
        columns = pl.ds(pl.multiple_of(block_at(place) * width, width), width)
        tails = unpack(source, limits[0], limits[1])
        for a in range(2):
            out[a, 0:main, columns] = source[a * main:(a + 1) * main]
            out[a, main:, columns] = tails[a]

    deliver(last.at[spot], spot)
    for step in range(1, n_state):
        place = lax.rem(spot + step, n_state)
        pltpu.make_async_remote_copy(
            src_ref=last.at[0],
            dst_ref=homed.at[place],
            send_sem=out_send.at[place],
            recv_sem=out_recv.at[place],
            device_id=(me, place),
            device_id_type=MESH,
        ).wait_recv()
        deliver(homed.at[place], place)
        out_copy(place).wait_send()
        a2a_copy(place).wait_send()
    for level in range(DEG):
        for piece in range(half):
            far_copy(level, piece).wait_send()
            near_copy(level, piece).wait_send()


def on_device(n_elem, n_state, orbitals, rotation, counts, neighbors, blocks):
    pair, rows, states = orbitals.shape
    elems = counts.shape[0]
    width = states // n_state
    packed = 2 * rows - 32
    dma = pltpu.SemaphoreType.DMA
    return pl.pallas_call(
        functools.partial(kernel, n_elem, n_state),
        out_shape=jax.ShapeDtypeStruct((pair, rows, states), jnp.bfloat16),
        in_specs=[pl.BlockSpec(memory_space=pltpu.HBM)] * 5,
        out_specs=pl.BlockSpec(memory_space=pltpu.VMEM),
        scratch_shapes=[
            pltpu.SMEM(counts.shape, jnp.int32),
            pltpu.SMEM(neighbors.shape[::-1], jnp.int32),
            pltpu.VMEM((pair * rows, states), jnp.bfloat16),
            pltpu.VMEM(rotation.shape, jnp.bfloat16),
            dma((4,)),
            dma((n_state,)),
            pltpu.VMEM((DEG, elems + 8, rows, width), jnp.bfloat16),
            pltpu.VMEM((DEG, 2, packed, width), jnp.bfloat16),
            pltpu.VMEM((DEG, 2, packed, width), jnp.bfloat16),
            pltpu.VMEM((DEG, 4, rows, width), jnp.bfloat16),
            pltpu.VMEM((n_state, packed, width), jnp.bfloat16),
            pltpu.VMEM((n_state, packed, width), jnp.bfloat16),
            pltpu.VMEM((n_state, packed, width), jnp.bfloat16),
            pltpu.VMEM((n_state, packed, width), jnp.bfloat16),
            pltpu.VMEM(blocks.shape, jnp.bfloat16),
            pltpu.VMEM((2, rows, width), jnp.bfloat16),
            pltpu.VMEM((4, 8, width), jnp.int32),
            pltpu.VMEM((4, 8, width), jnp.int32),
            dma,
            dma,
            dma((n_state,)),
            dma((n_state,)),
            dma((DEG, 2)),
            dma((DEG, 2)),
            dma((DEG, 2)),
            dma((DEG, 2)),
            dma((n_state,)),
            dma((n_state,)),
        ],
        compiler_params=pltpu.CompilerParams(
            collective_id=0, has_side_effects=True, vmem_limit_bytes=48 * 1024 * 1024
        ),
    )(*[
        pltpu.with_memory_space_constraint(x, pltpu.HBM)
        for x in (counts, neighbors.T, orbitals.reshape(pair * rows, states), rotation, blocks)
    ])


def solution(mesh):
    n_elem, n_state = mesh.shape["elem"], mesh.shape["state"]
    in_specs = (
        P(("elem", "state"), None, None),
        P(),
        P("elem"),
        P("elem", None),
        P("elem", None, None, None),
    )
    return jax.shard_map(
        functools.partial(on_device, n_elem, n_state),
        mesh=mesh,
        in_specs=in_specs,
        out_specs=P(("elem", "state"), None, None),
        check_vma=False,
    )
```

```python
import functools

import jax
import jax.numpy as jnp
from jax import lax
from jax.experimental import pallas as pl
from jax.experimental.pallas import tpu as pltpu
from jax.sharding import PartitionSpec as P

MESH = pl.DeviceIdType.MESH
DEG = 4
center_shift = 0.2
half_span = 1.1


def kernel(
    n_elem, n_state, counts_hbm, neighbors_hbm, orbitals_hbm, rotation_hbm, blocks_hbm, out,
    counts, neighbors, orbitals, rotation, load_sem, column_sem, fields, far_out, far_halo, near_halo, last,
    staged, landed, homed, blocks, scratch, own_counts, far_counts, count_send, count_recv,
    a2a_send, a2a_recv, far_send, far_recv, near_send, near_recv, out_send, out_recv,
):
    me, spot = lax.axis_index("elem"), lax.axis_index("state")
    core = lax.rem(me, 2)
    high = lax.rem(me // 2, 2)
    elems, reach = counts.shape[0], 4
    half = reach // 2
    rows, width = fields.shape[2], fields.shape[3]
    total = n_elem * elems

    def block_at(place):
        return jnp.where(high == 0, place, n_state - 1 - place)

    mine = block_at(spot)
    far = lax.rem(me + jnp.where(core == 0, n_elem - 1, 1), n_elem)
    far_id = (far, n_state - 1 - spot)
    near_id = (me + 1 - 2 * core, spot)

    def column_load(place):
        columns = pl.ds(pl.multiple_of(block_at(place) * width, width), width)
        return pltpu.make_async_copy(
            rotation_hbm.at[:, columns], rotation.at[:, columns], column_sem.at[place]
        )

    furthest = jnp.where(spot < n_state // 2, n_state - 1, 0)
    loads = [
        pltpu.make_async_copy(source, target, load_sem.at[i])
        for i, (source, target) in enumerate([
            (counts_hbm, counts), (orbitals_hbm, orbitals),
            (neighbors_hbm, neighbors), (blocks_hbm, blocks),
        ])
    ]
    column_load(furthest).start()
    for load in loads[:2]:
        load.start()
    for step in range(1, n_state):
        column_load(lax.rem(furthest + step, n_state)).start()

    barrier = pltpu.get_barrier_semaphore()
    for step in range(1, n_state):
        pl.semaphore_signal(
            barrier, inc=1, device_id=(me, lax.rem(spot + step, n_state)), device_id_type=MESH
        )
    for device in (far_id, near_id):
        pl.semaphore_signal(barrier, inc=1, device_id=device, device_id_type=MESH)

    for load in loads[:2]:
        load.wait()
    row = lax.broadcasted_iota(jnp.int32, (rows, width), 0)
    main = 128
    tail = rows - main
    tail_row = row[:tail]
    flip = (
        lax.broadcasted_iota(jnp.int32, (tail, tail), 0)
        + lax.broadcasted_iota(jnp.int32, (tail, tail), 1)
        == tail - 1
    ).astype(jnp.bfloat16)

    def flipped(part):
        return jnp.dot(flip, part, preferred_element_type=jnp.float32).astype(jnp.bfloat16)

    def pack(target, first, second):
        target[0:main] = first[:main]
        target[main:2 * main] = second[:main]
        target[2 * main:] = first[main:] + flipped(second[main:])

    def unpack(source, limit_first, limit_second):
        shared = source[2 * main:]
        zero = jnp.zeros_like(shared)
        return (
            jnp.where(tail_row < limit_first - main, shared, zero),
            jnp.where(tail_row < limit_second - main, flipped(shared), zero),
        )

    def a2a_copy(place):
        return pltpu.make_async_remote_copy(
            src_ref=staged.at[place],
            dst_ref=landed.at[spot],
            send_sem=a2a_send.at[place],
            recv_sem=a2a_recv.at[spot],
            device_id=(me, place),
            device_id_type=MESH,
        )

    limits = [counts[2 * spot], counts[2 * spot + 1]]

    def stage(place):
        columns = pl.ds(pl.multiple_of(block_at(place) * width, width), width)
        column_load(place).wait()
        result = jnp.dot(
            orbitals[...], rotation[:, columns], preferred_element_type=jnp.float32
        )
        first, second = [
            jnp.where(row < limits[a], result[a * rows:(a + 1) * rows], 0.0).astype(jnp.bfloat16)
            for a in range(2)
        ]
        pack(staged.at[place], first, second)

    far_own = jnp.where(core == 0, 0, elems - reach)
    for j in range(reach):
        own_counts[j] = jnp.full((8, width), counts[far_own + j], jnp.int32)
    count_copy = pltpu.make_async_remote_copy(
        src_ref=own_counts,
        dst_ref=far_counts,
        send_sem=count_send,
        recv_sem=count_recv,
        device_id=far_id,
        device_id_type=MESH,
    )
    stage(furthest)
    for load in loads[2:]:
        load.start()
    pl.semaphore_wait(barrier, n_state + 1)
    a2a_copy(furthest).start()
    count_copy.start()

    @pl.loop(1, 2 * n_state - 2)
    def _(step):
        distance = n_state - 1 - step // 2
        side = jnp.where(spot < n_state // 2, 1, -1) * (1 - 2 * lax.rem(step, 2))
        place = spot + side * distance

        @pl.when((place >= 0) & (place < n_state) & (place != furthest))
        def _():
            stage(place)
            a2a_copy(place).start()

    stage(spot)

    def arrived(pair):
        @pl.when(pair != spot)
        def _():
            pltpu.make_async_remote_copy(
                src_ref=staged.at[0],
                dst_ref=landed.at[pair],
                send_sem=a2a_send.at[0],
                recv_sem=a2a_recv.at[pair],
                device_id=(me, pair),
                device_id_type=MESH,
            ).wait_recv()

        @pl.when(pair == spot)
        def _():
            landed[pair] = staged[pair]

    def settle(pair):
        fields_pair(landed.at[pair], 0, reach + 2 * pair, counts[2 * pair], counts[2 * pair + 1])

    def fields_pair(source, level, slot, limit_first, limit_second):
        tails = unpack(source, limit_first, limit_second)
        for a in range(2):
            fields[level, slot + a, 0:main] = source[a * main:(a + 1) * main]
            fields[level, slot + a, main:] = tails[a]

    near_own = jnp.where(core == 0, elems - reach, 0)
    far_slot = jnp.where(core == 0, 0, elems + reach)
    near_slot = jnp.where(core == 0, elems + reach, 0)

    def far_copy(level, piece):
        return pltpu.make_async_remote_copy(
            src_ref=landed.at[far_own // 2 + piece] if level == 0 else far_out.at[level, piece],
            dst_ref=far_halo.at[level, piece],
            send_sem=far_send.at[level, piece],
            recv_sem=far_recv.at[level, piece],
            device_id=far_id,
            device_id_type=MESH,
        )

    def near_copy(level, piece):
        return pltpu.make_async_remote_copy(
            src_ref=fields.at[level, pl.ds(reach + near_own + 2 * piece, 2)],
            dst_ref=near_halo.at[level, pl.ds(2 * piece, 2)],
            send_sem=near_send.at[level, piece],
            recv_sem=near_recv.at[level, piece],
            device_id=near_id,
            device_id_type=MESH,
        )

    outer, inner = core, 1 - core
    for piece in (inner, outer):
        arrived(far_own // 2 + piece)
        far_copy(0, piece).start()
    for piece in range(half):
        pair = near_own // 2 + piece
        arrived(pair)
        settle(pair)
        near_copy(0, piece).start()
    for piece in range(half):
        settle(far_own // 2 + piece)
    for pair in range(half, elems // 2 - half):
        arrived(pair)
        settle(pair)
    count_copy.wait()
    for load in loads[2:]:
        load.wait()

    start_of_all = me * elems - reach

    def updated(level, e):
        image = jnp.zeros((rows, width), jnp.float32)
        for k in range(5):
            source = neighbors[k, e] - start_of_all
            source = jnp.where(source < 0, source + total, source)
            source = jnp.where(source >= total, source - total, source)
            source = jnp.clip(source, 0, elems + 2 * reach - 1)
            image += jnp.dot(
                blocks[e, k], fields[level - 1, source], preferred_element_type=jnp.float32
            )
        image = jnp.where(row < counts[e], image, 0.0)
        current = fields[level - 1, reach + e].astype(jnp.float32)
        factor = (1.0 if level == 1 else 2.0) / half_span
        value = factor * (image - center_shift * current)
        if level > 1:
            value = value - fields[level - 2, reach + e].astype(jnp.float32)
        return value.astype(jnp.bfloat16)

    def pair_of(level, pair):
        if level < DEG:
            @pl.loop(0, 2)
            def _(a):
                e = 2 * pair + a
                fields[level, reach + e] = updated(level, e)
        else:
            @pl.loop(0, 2)
            def _(a):
                scratch[a] = updated(level, 2 * pair + a)

            pack(last.at[pair], scratch[0], scratch[1])

    def out_copy(pair):
        return pltpu.make_async_remote_copy(
            src_ref=last.at[pair],
            dst_ref=homed.at[spot],
            send_sem=out_send.at[pair],
            recv_sem=out_recv.at[spot],
            device_id=(me, pair),
            device_id_type=MESH,
        )

    def ship(pair):
        @pl.when(pair != spot)
        def _():
            out_copy(pair).start()

    def receive(level, piece):
        far_copy(level, piece).wait_recv()
        fields_pair(
            far_halo.at[level, piece],
            level,
            far_slot + 2 * piece,
            far_counts[2 * piece, 0:1],
            far_counts[2 * piece + 1, 0:1],
        )

    def produce(level, piece):
        pair = far_own // 2 + piece
        pair_of(level, pair)
        if level < DEG:
            slot = reach + 2 * pair
            pack(far_out.at[level, piece], fields[level, slot], fields[level, slot + 1])
            far_copy(level, piece).start()
        else:
            ship(pair)

    for level in range(1, DEG + 1):
        for piece in range(half):
            near_copy(level - 1, piece).wait_recv()
        fields[level - 1, pl.ds(near_slot, reach)] = near_halo[level - 1]
        for piece in range(half):
            pair = near_own // 2 + piece
            pair_of(level, pair)
            if level < DEG:
                near_copy(level, piece).start()
            else:
                ship(pair)
        for pair in range(half, elems // 2 - half):
            pair_of(level, pair)
            if level == DEG:
                ship(pair)
        if level % 2 == 0:
            receive(level - 1, inner)
            produce(level, inner)
            receive(level - 1, outer)
            produce(level, outer)
        else:
            receive(level - 1, outer)
            receive(level - 1, inner)
            produce(level, outer)
            produce(level, inner)

    def deliver(source, place):
        columns = pl.ds(pl.multiple_of(block_at(place) * width, width), width)
        tails = unpack(source, limits[0], limits[1])
        for a in range(2):
            out[a, 0:main, columns] = source[a * main:(a + 1) * main]
            out[a, main:, columns] = tails[a]

    deliver(last.at[spot], spot)
    for step in range(1, n_state):
        place = lax.rem(spot + step, n_state)
        pltpu.make_async_remote_copy(
            src_ref=last.at[0],
            dst_ref=homed.at[place],
            send_sem=out_send.at[place],
            recv_sem=out_recv.at[place],
            device_id=(me, place),
            device_id_type=MESH,
        ).wait_recv()
        deliver(homed.at[place], place)
        out_copy(place).wait_send()
        a2a_copy(place).wait_send()
    for level in range(DEG):
        for piece in range(half):
            far_copy(level, piece).wait_send()
            near_copy(level, piece).wait_send()


def on_device(n_elem, n_state, orbitals, rotation, counts, neighbors, blocks):
    pair, rows, states = orbitals.shape
    elems = counts.shape[0]
    width = states // n_state
    packed = 2 * rows - 32
    dma = pltpu.SemaphoreType.DMA
    return pl.pallas_call(
        functools.partial(kernel, n_elem, n_state),
        out_shape=jax.ShapeDtypeStruct((pair, rows, states), jnp.bfloat16),
        in_specs=[pl.BlockSpec(memory_space=pltpu.HBM)] * 5,
        out_specs=pl.BlockSpec(memory_space=pltpu.VMEM),
        scratch_shapes=[
            pltpu.SMEM(counts.shape, jnp.int32),
            pltpu.SMEM(neighbors.shape[::-1], jnp.int32),
            pltpu.VMEM((pair * rows, states), jnp.bfloat16),
            pltpu.VMEM(rotation.shape, jnp.bfloat16),
            dma((4,)),
            dma((n_state,)),
            pltpu.VMEM((DEG, elems + 8, rows, width), jnp.bfloat16),
            pltpu.VMEM((DEG, 2, packed, width), jnp.bfloat16),
            pltpu.VMEM((DEG, 2, packed, width), jnp.bfloat16),
            pltpu.VMEM((DEG, 4, rows, width), jnp.bfloat16),
            pltpu.VMEM((n_state, packed, width), jnp.bfloat16),
            pltpu.VMEM((n_state, packed, width), jnp.bfloat16),
            pltpu.VMEM((n_state, packed, width), jnp.bfloat16),
            pltpu.VMEM((n_state, packed, width), jnp.bfloat16),
            pltpu.VMEM(blocks.shape, jnp.bfloat16),
            pltpu.VMEM((2, rows, width), jnp.bfloat16),
            pltpu.VMEM((4, 8, width), jnp.int32),
            pltpu.VMEM((4, 8, width), jnp.int32),
            dma,
            dma,
            dma((n_state,)),
            dma((n_state,)),
            dma((DEG, 2)),
            dma((DEG, 2)),
            dma((DEG, 2)),
            dma((DEG, 2)),
            dma((n_state,)),
            dma((n_state,)),
        ],
        compiler_params=pltpu.CompilerParams(
            collective_id=0, has_side_effects=True, vmem_limit_bytes=48 * 1024 * 1024
        ),
    )(*[
        pltpu.with_memory_space_constraint(x, pltpu.HBM)
        for x in (counts, neighbors.T, orbitals.reshape(pair * rows, states), rotation, blocks)
    ])


def solution(mesh):
    n_elem, n_state = mesh.shape["elem"], mesh.shape["state"]
    in_specs = (
        P(("elem", "state"), None, None),
        P(),
        P("elem"),
        P("elem", None),
        P("elem", None, None, None),
    )
    return jax.shard_map(
        functools.partial(on_device, n_elem, n_state),
        mesh=mesh,
        in_specs=in_specs,
        out_specs=P(("elem", "state"), None, None),
        check_vma=False,
    )
```

```python
import functools

import jax
import jax.numpy as jnp
from jax import lax
from jax.experimental import pallas as pl
from jax.experimental.pallas import tpu as pltpu
from jax.sharding import PartitionSpec as P

MESH = pl.DeviceIdType.MESH
DEG = 4
center_shift = 0.2
half_span = 1.1


def kernel(
    n_elem, n_state, counts_hbm, neighbors_hbm, orbitals_hbm, rotation_hbm, blocks_hbm, out,
    counts, neighbors, orbitals, rotation, load_sem, column_sem, fields, far_out, far_halo, near_halo, last,
    staged, landed, homed, blocks, scratch, own_counts, far_counts, count_send, count_recv,
    a2a_send, a2a_recv, far_send, far_recv, near_send, near_recv, out_send, out_recv,
):
    me, spot = lax.axis_index("elem"), lax.axis_index("state")
    core = lax.rem(me, 2)
    high = lax.rem(me // 2, 2)
    elems, reach = counts.shape[0], 4
    half = reach // 2
    rows, width = fields.shape[2], fields.shape[3]
    total = n_elem * elems

    def block_at(place):
        return jnp.where(high == 0, place, n_state - 1 - place)

    mine = block_at(spot)
    far = lax.rem(me + jnp.where(core == 0, n_elem - 1, 1), n_elem)
    far_id = (far, n_state - 1 - spot)
    near_id = (me + 1 - 2 * core, spot)

    def column_load(place):
        columns = pl.ds(pl.multiple_of(block_at(place) * width, width), width)
        return pltpu.make_async_copy(
            rotation_hbm.at[:, columns], rotation.at[:, columns], column_sem.at[place]
        )

    furthest = jnp.where(spot < n_state // 2, n_state - 1, 0)
    loads = [
        pltpu.make_async_copy(source, target, load_sem.at[i])
        for i, (source, target) in enumerate([
            (counts_hbm, counts), (orbitals_hbm, orbitals),
            (neighbors_hbm, neighbors), (blocks_hbm, blocks),
        ])
    ]
    column_load(furthest).start()
    for load in loads[:2]:
        load.start()
    for step in range(1, n_state):
        column_load(lax.rem(furthest + step, n_state)).start()

    barrier = pltpu.get_barrier_semaphore()
    for step in range(1, n_state):
        pl.semaphore_signal(
            barrier, inc=1, device_id=(me, lax.rem(spot + step, n_state)), device_id_type=MESH
        )
    for device in (far_id, near_id):
        pl.semaphore_signal(barrier, inc=1, device_id=device, device_id_type=MESH)

    for load in loads[:2]:
        load.wait()
    row = lax.broadcasted_iota(jnp.int32, (rows, width), 0)
    main = 128
    tail = rows - main
    tail_row = row[:tail]
    flip = (
        lax.broadcasted_iota(jnp.int32, (tail, tail), 0)
        + lax.broadcasted_iota(jnp.int32, (tail, tail), 1)
        == tail - 1
    ).astype(jnp.bfloat16)

    def flipped(part):
        return jnp.dot(flip, part, preferred_element_type=jnp.float32).astype(jnp.bfloat16)

    def pack(target, first, second):
        target[0:main] = first[:main]
        target[main:2 * main] = second[:main]
        target[2 * main:] = first[main:] + flipped(second[main:])

    def unpack(source, limit_first, limit_second):
        shared = source[2 * main:]
        zero = jnp.zeros_like(shared)
        return (
            jnp.where(tail_row < limit_first - main, shared, zero),
            jnp.where(tail_row < limit_second - main, flipped(shared), zero),
        )

    def a2a_copy(place):
        return pltpu.make_async_remote_copy(
            src_ref=staged.at[place],
            dst_ref=landed.at[spot],
            send_sem=a2a_send.at[place],
            recv_sem=a2a_recv.at[spot],
            device_id=(me, place),
            device_id_type=MESH,
        )

    limits = [counts[2 * spot], counts[2 * spot + 1]]

    def stage(place):
        columns = pl.ds(pl.multiple_of(block_at(place) * width, width), width)
        column_load(place).wait()
        result = jnp.dot(
            orbitals[...], rotation[:, columns], preferred_element_type=jnp.float32
        )
        first, second = [
            jnp.where(row < limits[a], result[a * rows:(a + 1) * rows], 0.0).astype(jnp.bfloat16)
            for a in range(2)
        ]
        pack(staged.at[place], first, second)

    far_own = jnp.where(core == 0, 0, elems - reach)
    for j in range(reach):
        own_counts[j] = jnp.full((8, width), counts[far_own + j], jnp.int32)
    count_copy = pltpu.make_async_remote_copy(
        src_ref=own_counts,
        dst_ref=far_counts,
        send_sem=count_send,
        recv_sem=count_recv,
        device_id=far_id,
        device_id_type=MESH,
    )
    stage(furthest)
    for load in loads[2:]:
        load.start()
    pl.semaphore_wait(barrier, n_state + 1)
    a2a_copy(furthest).start()
    count_copy.start()

    @pl.loop(1, 2 * n_state - 2)
    def _(step):
        distance = n_state - 1 - step // 2
        side = jnp.where(spot < n_state // 2, 1, -1) * (1 - 2 * lax.rem(step, 2))
        place = spot + side * distance

        @pl.when((place >= 0) & (place < n_state) & (place != furthest))
        def _():
            stage(place)
            a2a_copy(place).start()

    stage(spot)

    def arrived(pair):
        @pl.when(pair != spot)
        def _():
            pltpu.make_async_remote_copy(
                src_ref=staged.at[0],
                dst_ref=landed.at[pair],
                send_sem=a2a_send.at[0],
                recv_sem=a2a_recv.at[pair],
                device_id=(me, pair),
                device_id_type=MESH,
            ).wait_recv()

        @pl.when(pair == spot)
        def _():
            landed[pair] = staged[pair]

    def settle(pair):
        fields_pair(landed.at[pair], 0, reach + 2 * pair, counts[2 * pair], counts[2 * pair + 1])

    def fields_pair(source, level, slot, limit_first, limit_second):
        tails = unpack(source, limit_first, limit_second)
        for a in range(2):
            fields[level, slot + a, 0:main] = source[a * main:(a + 1) * main]
            fields[level, slot + a, main:] = tails[a]

    near_own = jnp.where(core == 0, elems - reach, 0)
    far_slot = jnp.where(core == 0, 0, elems + reach)
    near_slot = jnp.where(core == 0, elems + reach, 0)

    def far_copy(level, piece):
        return pltpu.make_async_remote_copy(
            src_ref=landed.at[far_own // 2 + piece] if level == 0 else far_out.at[level, piece],
            dst_ref=far_halo.at[level, piece],
            send_sem=far_send.at[level, piece],
            recv_sem=far_recv.at[level, piece],
            device_id=far_id,
            device_id_type=MESH,
        )

    def near_copy(level, piece):
        return pltpu.make_async_remote_copy(
            src_ref=fields.at[level, pl.ds(reach + near_own + 2 * piece, 2)],
            dst_ref=near_halo.at[level, pl.ds(2 * piece, 2)],
            send_sem=near_send.at[level, piece],
            recv_sem=near_recv.at[level, piece],
            device_id=near_id,
            device_id_type=MESH,
        )

    outer, inner = core, 1 - core
    for piece in (inner, outer):
        arrived(far_own // 2 + piece)
        far_copy(0, piece).start()
    for piece in range(half):
        pair = near_own // 2 + piece
        arrived(pair)
        settle(pair)
        near_copy(0, piece).start()
    for piece in range(half):
        settle(far_own // 2 + piece)
    for pair in range(half, elems // 2 - half):
        arrived(pair)
        settle(pair)
    count_copy.wait()
    for load in loads[2:]:
        load.wait()

    start_of_all = me * elems - reach

    def updated(level, e):
        image = jnp.zeros((rows, width), jnp.float32)
        for k in range(5):
            source = neighbors[k, e] - start_of_all
            source = jnp.where(source < 0, source + total, source)
            source = jnp.where(source >= total, source - total, source)
            source = jnp.clip(source, 0, elems + 2 * reach - 1)
            image += jnp.dot(
                blocks[e, k], fields[level - 1, source], preferred_element_type=jnp.float32
            )
        image = jnp.where(row < counts[e], image, 0.0)
        current = fields[level - 1, reach + e].astype(jnp.float32)
        factor = (1.0 if level == 1 else 2.0) / half_span
        value = factor * (image - center_shift * current)
        if level > 1:
            value = value - fields[level - 2, reach + e].astype(jnp.float32)
        return value.astype(jnp.bfloat16)

    def pair_of(level, pair):
        if level < DEG:
            values = [updated(level, 2 * pair + a) for a in range(2)]
            for a in range(2):
                fields[level, reach + 2 * pair + a] = values[a]
        else:
            values = [updated(level, 2 * pair + a) for a in range(2)]
            for a in range(2):
                scratch[a] = values[a]

            pack(last.at[pair], scratch[0], scratch[1])

    def out_copy(pair):
        return pltpu.make_async_remote_copy(
            src_ref=last.at[pair],
            dst_ref=homed.at[spot],
            send_sem=out_send.at[pair],
            recv_sem=out_recv.at[spot],
            device_id=(me, pair),
            device_id_type=MESH,
        )

    def ship(pair):
        @pl.when(pair != spot)
        def _():
            out_copy(pair).start()

    def receive(level, piece):
        far_copy(level, piece).wait_recv()
        fields_pair(
            far_halo.at[level, piece],
            level,
            far_slot + 2 * piece,
            far_counts[2 * piece, 0:1],
            far_counts[2 * piece + 1, 0:1],
        )

    def produce(level, piece):
        pair = far_own // 2 + piece
        pair_of(level, pair)
        if level < DEG:
            slot = reach + 2 * pair
            pack(far_out.at[level, piece], fields[level, slot], fields[level, slot + 1])
            far_copy(level, piece).start()
        else:
            ship(pair)

    for level in range(1, DEG + 1):
        for pair in range(half, elems // 2 - half):
            pair_of(level, pair)
            if level == DEG:
                ship(pair)
        for piece in range(half):
            near_copy(level - 1, piece).wait_recv()
        fields[level - 1, pl.ds(near_slot, reach)] = near_halo[level - 1]
        for piece in range(half):
            pair = near_own // 2 + piece
            pair_of(level, pair)
            if level < DEG:
                near_copy(level, piece).start()
            else:
                ship(pair)
        if level % 2 == 0:
            receive(level - 1, inner)
            produce(level, inner)
            receive(level - 1, outer)
            produce(level, outer)
        else:
            receive(level - 1, outer)
            receive(level - 1, inner)
            produce(level, outer)
            produce(level, inner)

    def deliver(source, place):
        columns = pl.ds(pl.multiple_of(block_at(place) * width, width), width)
        tails = unpack(source, limits[0], limits[1])
        for a in range(2):
            out[a, 0:main, columns] = source[a * main:(a + 1) * main]
            out[a, main:, columns] = tails[a]

    deliver(last.at[spot], spot)
    for step in range(1, n_state):
        place = lax.rem(spot + step, n_state)
        pltpu.make_async_remote_copy(
            src_ref=last.at[0],
            dst_ref=homed.at[place],
            send_sem=out_send.at[place],
            recv_sem=out_recv.at[place],
            device_id=(me, place),
            device_id_type=MESH,
        ).wait_recv()
        deliver(homed.at[place], place)
        out_copy(place).wait_send()
        a2a_copy(place).wait_send()
    for level in range(DEG):
        for piece in range(half):
            far_copy(level, piece).wait_send()
            near_copy(level, piece).wait_send()


def on_device(n_elem, n_state, orbitals, rotation, counts, neighbors, blocks):
    pair, rows, states = orbitals.shape
    elems = counts.shape[0]
    width = states // n_state
    packed = 2 * rows - 32
    dma = pltpu.SemaphoreType.DMA
    return pl.pallas_call(
        functools.partial(kernel, n_elem, n_state),
        out_shape=jax.ShapeDtypeStruct((pair, rows, states), jnp.bfloat16),
        in_specs=[pl.BlockSpec(memory_space=pltpu.HBM)] * 5,
        out_specs=pl.BlockSpec(memory_space=pltpu.VMEM),
        scratch_shapes=[
            pltpu.SMEM(counts.shape, jnp.int32),
            pltpu.SMEM(neighbors.shape[::-1], jnp.int32),
            pltpu.VMEM((pair * rows, states), jnp.bfloat16),
            pltpu.VMEM(rotation.shape, jnp.bfloat16),
            dma((4,)),
            dma((n_state,)),
            pltpu.VMEM((DEG, elems + 8, rows, width), jnp.bfloat16),
            pltpu.VMEM((DEG, 2, packed, width), jnp.bfloat16),
            pltpu.VMEM((DEG, 2, packed, width), jnp.bfloat16),
            pltpu.VMEM((DEG, 4, rows, width), jnp.bfloat16),
            pltpu.VMEM((n_state, packed, width), jnp.bfloat16),
            pltpu.VMEM((n_state, packed, width), jnp.bfloat16),
            pltpu.VMEM((n_state, packed, width), jnp.bfloat16),
            pltpu.VMEM((n_state, packed, width), jnp.bfloat16),
            pltpu.VMEM(blocks.shape, jnp.bfloat16),
            pltpu.VMEM((2, rows, width), jnp.bfloat16),
            pltpu.VMEM((4, 8, width), jnp.int32),
            pltpu.VMEM((4, 8, width), jnp.int32),
            dma,
            dma,
            dma((n_state,)),
            dma((n_state,)),
            dma((DEG, 2)),
            dma((DEG, 2)),
            dma((DEG, 2)),
            dma((DEG, 2)),
            dma((n_state,)),
            dma((n_state,)),
        ],
        compiler_params=pltpu.CompilerParams(
            collective_id=0, has_side_effects=True, vmem_limit_bytes=48 * 1024 * 1024
        ),
    )(*[
        pltpu.with_memory_space_constraint(x, pltpu.HBM)
        for x in (counts, neighbors.T, orbitals.reshape(pair * rows, states), rotation, blocks)
    ])


def solution(mesh):
    n_elem, n_state = mesh.shape["elem"], mesh.shape["state"]
    in_specs = (
        P(("elem", "state"), None, None),
        P(),
        P("elem"),
        P("elem", None),
        P("elem", None, None, None),
    )
    return jax.shard_map(
        functools.partial(on_device, n_elem, n_state),
        mesh=mesh,
        in_specs=in_specs,
        out_specs=P(("elem", "state"), None, None),
        check_vma=False,
    )
```

```python
import functools

import jax
import jax.numpy as jnp
from jax import lax
from jax.experimental import pallas as pl
from jax.experimental.pallas import tpu as pltpu
from jax.sharding import PartitionSpec as P

MESH = pl.DeviceIdType.MESH
DEG = 4
center_shift = 0.2
half_span = 1.1


def kernel(
    n_elem, n_state, counts_hbm, neighbors_hbm, orbitals_hbm, rotation_hbm, blocks_hbm, out,
    counts, neighbors, orbitals, rotation, load_sem, column_sem, fields, far_out, far_halo, near_halo, last,
    staged, landed, homed, blocks, scratch, own_counts, far_counts, count_send, count_recv,
    a2a_send, a2a_recv, far_send, far_recv, near_send, near_recv, out_send, out_recv,
):
    me, spot = lax.axis_index("elem"), lax.axis_index("state")
    core = lax.rem(me, 2)
    high = lax.rem(me // 2, 2)
    elems, reach = counts.shape[0], 4
    half = reach // 2
    rows, width = fields.shape[2], fields.shape[3]
    total = n_elem * elems

    def block_at(place):
        return jnp.where(high == 0, place, n_state - 1 - place)

    mine = block_at(spot)
    far = lax.rem(me + jnp.where(core == 0, n_elem - 1, 1), n_elem)
    far_id = (far, n_state - 1 - spot)
    near_id = (me + 1 - 2 * core, spot)

    def column_load(place):
        columns = pl.ds(pl.multiple_of(block_at(place) * width, width), width)
        return pltpu.make_async_copy(
            rotation_hbm.at[:, columns], rotation.at[:, columns], column_sem.at[place]
        )

    furthest = jnp.where(spot < n_state // 2, n_state - 1, 0)
    loads = [
        pltpu.make_async_copy(source, target, load_sem.at[i])
        for i, (source, target) in enumerate([
            (counts_hbm, counts), (orbitals_hbm, orbitals),
            (neighbors_hbm, neighbors), (blocks_hbm, blocks),
        ])
    ]
    column_load(furthest).start()
    for load in loads[:2]:
        load.start()
    for step in range(1, n_state):
        column_load(lax.rem(furthest + step, n_state)).start()

    barrier = pltpu.get_barrier_semaphore()
    for step in range(1, n_state):
        pl.semaphore_signal(
            barrier, inc=1, device_id=(me, lax.rem(spot + step, n_state)), device_id_type=MESH
        )
    for device in (far_id, near_id):
        pl.semaphore_signal(barrier, inc=1, device_id=device, device_id_type=MESH)

    for load in loads[:2]:
        load.wait()
    row = lax.broadcasted_iota(jnp.int32, (rows, width), 0)
    main = 128
    tail = rows - main
    tail_row = row[:tail]
    flip = (
        lax.broadcasted_iota(jnp.int32, (tail, tail), 0)
        + lax.broadcasted_iota(jnp.int32, (tail, tail), 1)
        == tail - 1
    ).astype(jnp.bfloat16)

    def flipped(part):
        return jnp.dot(flip, part, preferred_element_type=jnp.float32).astype(jnp.bfloat16)

    def pack(target, first, second):
        target[0:main] = first[:main]
        target[main:2 * main] = second[:main]
        target[2 * main:] = first[main:] + flipped(second[main:])

    def unpack(source, limit_first, limit_second):
        shared = source[2 * main:]
        zero = jnp.zeros_like(shared)
        return (
            jnp.where(tail_row < limit_first - main, shared, zero),
            jnp.where(tail_row < limit_second - main, flipped(shared), zero),
        )

    def a2a_copy(place):
        return pltpu.make_async_remote_copy(
            src_ref=staged.at[place],
            dst_ref=landed.at[spot],
            send_sem=a2a_send.at[place],
            recv_sem=a2a_recv.at[spot],
            device_id=(me, place),
            device_id_type=MESH,
        )

    limits = [counts[2 * spot], counts[2 * spot + 1]]

    def stage(place):
        columns = pl.ds(pl.multiple_of(block_at(place) * width, width), width)
        column_load(place).wait()
        result = jnp.dot(
            orbitals[...], rotation[:, columns], preferred_element_type=jnp.float32
        )
        first, second = [
            jnp.where(row < limits[a], result[a * rows:(a + 1) * rows], 0.0).astype(jnp.bfloat16)
            for a in range(2)
        ]
        pack(staged.at[place], first, second)

    far_own = jnp.where(core == 0, 0, elems - reach)
    for j in range(reach):
        own_counts[j] = jnp.full((8, width), counts[far_own + j], jnp.int32)
    count_copy = pltpu.make_async_remote_copy(
        src_ref=own_counts,
        dst_ref=far_counts,
        send_sem=count_send,
        recv_sem=count_recv,
        device_id=far_id,
        device_id_type=MESH,
    )
    stage(furthest)
    for load in loads[2:]:
        load.start()
    pl.semaphore_wait(barrier, n_state + 1)
    a2a_copy(furthest).start()
    count_copy.start()

    @pl.loop(1, 2 * n_state - 2)
    def _(step):
        distance = n_state - 1 - step // 2
        side = jnp.where(spot < n_state // 2, 1, -1) * (1 - 2 * lax.rem(step, 2))
        place = spot + side * distance

        @pl.when((place >= 0) & (place < n_state) & (place != furthest))
        def _():
            stage(place)
            a2a_copy(place).start()

    stage(spot)

    def arrived(pair):
        @pl.when(pair != spot)
        def _():
            pltpu.make_async_remote_copy(
                src_ref=staged.at[0],
                dst_ref=landed.at[pair],
                send_sem=a2a_send.at[0],
                recv_sem=a2a_recv.at[pair],
                device_id=(me, pair),
                device_id_type=MESH,
            ).wait_recv()

        @pl.when(pair == spot)
        def _():
            landed[pair] = staged[pair]

    def settle(pair):
        fields_pair(landed.at[pair], 0, reach + 2 * pair, counts[2 * pair], counts[2 * pair + 1])

    def fields_pair(source, level, slot, limit_first, limit_second):
        tails = unpack(source, limit_first, limit_second)
        for a in range(2):
            fields[level, slot + a, 0:main] = source[a * main:(a + 1) * main]
            fields[level, slot + a, main:] = tails[a]

    near_own = jnp.where(core == 0, elems - reach, 0)
    far_slot = jnp.where(core == 0, 0, elems + reach)
    near_slot = jnp.where(core == 0, elems + reach, 0)

    def far_copy(level, piece):
        return pltpu.make_async_remote_copy(
            src_ref=landed.at[far_own // 2 + piece] if level == 0 else far_out.at[level, piece],
            dst_ref=far_halo.at[level, piece],
            send_sem=far_send.at[level, piece],
            recv_sem=far_recv.at[level, piece],
            device_id=far_id,
            device_id_type=MESH,
        )

    def near_copy(level, piece):
        return pltpu.make_async_remote_copy(
            src_ref=fields.at[level, pl.ds(reach + near_own + 2 * piece, 2)],
            dst_ref=near_halo.at[level, pl.ds(2 * piece, 2)],
            send_sem=near_send.at[level, piece],
            recv_sem=near_recv.at[level, piece],
            device_id=near_id,
            device_id_type=MESH,
        )

    outer, inner = core, 1 - core
    for piece in (inner, outer):
        arrived(far_own // 2 + piece)
        far_copy(0, piece).start()
    for piece in range(half):
        pair = near_own // 2 + piece
        arrived(pair)
        settle(pair)
        near_copy(0, piece).start()
    for piece in range(half):
        settle(far_own // 2 + piece)
    for pair in range(half, elems // 2 - half):
        arrived(pair)
        settle(pair)
    count_copy.wait()
    for load in loads[2:]:
        load.wait()

    start_of_all = me * elems - reach

    def updated(level, e):
        image = jnp.zeros((rows, width), jnp.float32)
        for k in range(5):
            source = neighbors[k, e] - start_of_all
            source = jnp.where(source < 0, source + total, source)
            source = jnp.where(source >= total, source - total, source)
            source = jnp.clip(source, 0, elems + 2 * reach - 1)
            image += jnp.dot(
                blocks[e, k], fields[level - 1, source], preferred_element_type=jnp.float32
            )
        image = jnp.where(row < counts[e], image, 0.0)
        current = fields[level - 1, reach + e].astype(jnp.float32)
        factor = (1.0 if level == 1 else 2.0) / half_span
        value = factor * (image - center_shift * current)
        if level > 1:
            value = value - fields[level - 2, reach + e].astype(jnp.float32)
        return value.astype(jnp.bfloat16)

    def pair_of(level, pair):
        if level < DEG:
            @pl.loop(0, 2)
            def _(a):
                e = 2 * pair + a
                fields[level, reach + e] = updated(level, e)
        else:
            @pl.loop(0, 2)
            def _(a):
                scratch[a] = updated(level, 2 * pair + a)

            pack(last.at[pair], scratch[0], scratch[1])

    def out_copy(pair):
        return pltpu.make_async_remote_copy(
            src_ref=last.at[pair],
            dst_ref=homed.at[spot],
            send_sem=out_send.at[pair],
            recv_sem=out_recv.at[spot],
            device_id=(me, pair),
            device_id_type=MESH,
        )

    def ship(pair):
        @pl.when(pair != spot)
        def _():
            out_copy(pair).start()

    def receive(level, piece):
        far_copy(level, piece).wait_recv()
        fields_pair(
            far_halo.at[level, piece],
            level,
            far_slot + 2 * piece,
            far_counts[2 * piece, 0:1],
            far_counts[2 * piece + 1, 0:1],
        )

    def produce(level, piece):
        pair = far_own // 2 + piece
        pair_of(level, pair)
        if level < DEG:
            slot = reach + 2 * pair
            pack(far_out.at[level, piece], fields[level, slot], fields[level, slot + 1])
            far_copy(level, piece).start()
        else:
            ship(pair)

    for level in range(1, DEG + 1):
        for pair in range(half, elems // 2 - half):
            pair_of(level, pair)
            if level == DEG:
                ship(pair)
        for piece in range(half):
            near_copy(level - 1, piece).wait_recv()
        fields[level - 1, pl.ds(near_slot, reach)] = near_halo[level - 1]
        for piece in (inner, outer):
            pair = near_own // 2 + piece
            pair_of(level, pair)
            if level < DEG:
                near_copy(level, piece).start()
            else:
                ship(pair)
        if level % 2 == 0:
            receive(level - 1, inner)
            produce(level, inner)
            receive(level - 1, outer)
            produce(level, outer)
        else:
            receive(level - 1, outer)
            receive(level - 1, inner)
            produce(level, outer)
            produce(level, inner)

    def deliver(source, place):
        columns = pl.ds(pl.multiple_of(block_at(place) * width, width), width)
        tails = unpack(source, limits[0], limits[1])
        for a in range(2):
            out[a, 0:main, columns] = source[a * main:(a + 1) * main]
            out[a, main:, columns] = tails[a]

    deliver(last.at[spot], spot)
    for step in range(1, n_state):
        place = lax.rem(spot + step, n_state)
        pltpu.make_async_remote_copy(
            src_ref=last.at[0],
            dst_ref=homed.at[place],
            send_sem=out_send.at[place],
            recv_sem=out_recv.at[place],
            device_id=(me, place),
            device_id_type=MESH,
        ).wait_recv()
        deliver(homed.at[place], place)
        out_copy(place).wait_send()
        a2a_copy(place).wait_send()
    for level in range(DEG):
        for piece in range(half):
            far_copy(level, piece).wait_send()
            near_copy(level, piece).wait_send()


def on_device(n_elem, n_state, orbitals, rotation, counts, neighbors, blocks):
    pair, rows, states = orbitals.shape
    elems = counts.shape[0]
    width = states // n_state
    packed = 2 * rows - 32
    dma = pltpu.SemaphoreType.DMA
    return pl.pallas_call(
        functools.partial(kernel, n_elem, n_state),
        out_shape=jax.ShapeDtypeStruct((pair, rows, states), jnp.bfloat16),
        in_specs=[pl.BlockSpec(memory_space=pltpu.HBM)] * 5,
        out_specs=pl.BlockSpec(memory_space=pltpu.VMEM),
        scratch_shapes=[
            pltpu.SMEM(counts.shape, jnp.int32),
            pltpu.SMEM(neighbors.shape[::-1], jnp.int32),
            pltpu.VMEM((pair * rows, states), jnp.bfloat16),
            pltpu.VMEM(rotation.shape, jnp.bfloat16),
            dma((4,)),
            dma((n_state,)),
            pltpu.VMEM((DEG, elems + 8, rows, width), jnp.bfloat16),
            pltpu.VMEM((DEG, 2, packed, width), jnp.bfloat16),
            pltpu.VMEM((DEG, 2, packed, width), jnp.bfloat16),
            pltpu.VMEM((DEG, 4, rows, width), jnp.bfloat16),
            pltpu.VMEM((n_state, packed, width), jnp.bfloat16),
            pltpu.VMEM((n_state, packed, width), jnp.bfloat16),
            pltpu.VMEM((n_state, packed, width), jnp.bfloat16),
            pltpu.VMEM((n_state, packed, width), jnp.bfloat16),
            pltpu.VMEM(blocks.shape, jnp.bfloat16),
            pltpu.VMEM((2, rows, width), jnp.bfloat16),
            pltpu.VMEM((4, 8, width), jnp.int32),
            pltpu.VMEM((4, 8, width), jnp.int32),
            dma,
            dma,
            dma((n_state,)),
            dma((n_state,)),
            dma((DEG, 2)),
            dma((DEG, 2)),
            dma((DEG, 2)),
            dma((DEG, 2)),
            dma((n_state,)),
            dma((n_state,)),
        ],
        compiler_params=pltpu.CompilerParams(
            collective_id=0, has_side_effects=True, vmem_limit_bytes=48 * 1024 * 1024
        ),
    )(*[
        pltpu.with_memory_space_constraint(x, pltpu.HBM)
        for x in (counts, neighbors.T, orbitals.reshape(pair * rows, states), rotation, blocks)
    ])


def solution(mesh):
    n_elem, n_state = mesh.shape["elem"], mesh.shape["state"]
    in_specs = (
        P(("elem", "state"), None, None),
        P(),
        P("elem"),
        P("elem", None),
        P("elem", None, None, None),
    )
    return jax.shard_map(
        functools.partial(on_device, n_elem, n_state),
        mesh=mesh,
        in_specs=in_specs,
        out_specs=P(("elem", "state"), None, None),
        check_vma=False,
    )
```
